32 devices in a mesh: row: 2 (over y), col: 16 (over z, x, core).
Axes of the slice: x: 2, y: 2, z: 4, core: 2. Of those that a mesh axis runs over, the one named last changes fastest.
Arguments:
- w_slab: float32 [512, 16384], P('row', 'col'), may hold values from -0.25 to 0.25
- prior_cov: float32 [16384, 16384], P('row', 'col'), as said below
Outputs:
- posterior: float32 [16384, 16384], P('row', 'col')
The draws below stay inside these ranges and needn't reach their ends.
Inputs may be any that keep to these rules, and one draw needn't show every extreme that they name: prior_cov is symmetric.
All inputs are finite; a program needn't handle non-finite values.
Results may differ from the reference program's by a relative error of at most 0.00005.
Values sent between devices are 32-bit elements; how exact they have to be, the bound alone decides.
No kernel may reach another device: no remote copies, remote signals or barrier semaphores. Data moves between devices by JAX's collectives and lax.ppermute only.
A program may use at most 256 MiB of HBM per device.

```python
import jax
import jax.numpy as jnp
from jax import lax

NB = 16384
K = 512


def draw_prior_cov(key, part):
    first, second = jax.random.split(jax.random.fold_in(key, 11))
    index = jnp.arange(NB, dtype=jnp.float32)
    scales = jnp.exp(jax.random.uniform(first, (NB,), jnp.float32, -0.35, 0.35))
    noise = jax.random.uniform(second, (NB, NB), jnp.float32, -1.0, 1.0)
    decay = jnp.exp(-jnp.abs(index[:, None] - index[None, :]) / 64.0)
    return scales[:, None] * scales[None, :] * decay + 0.1 * (noise + noise.T)


def steps_of(own_key, shape, pieces, low, high):
    level, own = 1.0, jax.random.fold_in(own_key, 6)
    for dim, parts in pieces:
        steps = jnp.exp(jax.random.uniform(jax.random.fold_in(own, dim), (parts,), jnp.float32, low / len(pieces), high / len(pieces)))
        level = level * jnp.repeat(steps, shape[dim] // parts).reshape([-1 if axis == dim else 1 for axis in range(len(shape))])
    return level


def normal_values(rng, extent, width, limit, cuts=(), kind=jnp.bfloat16):
    values = width * jax.random.normal(rng, extent, jnp.float32)
    if cuts:
        values = values * steps_of(rng, extent, cuts, -0.22, 0.18)
    return jnp.clip(values, -limit, limit).astype(kind)


def setup_inputs(seed: int = 0) -> dict:
    keys = jax.random.split(jax.random.key(seed), 3)
    return {
        "w_slab": normal_values(keys[0], (K, NB), K ** -0.5, 0.25, ((0, 2), (1, 16)), jnp.float32),
        "prior_cov": draw_prior_cov(jax.random.fold_in(keys[2], 71), 0),
    }


def reference(w_slab, prior_cov):
    gram = lax.dot_general(w_slab, w_slab, (((0,), (0,)), ((), ())), precision=lax.Precision.HIGHEST, preferred_element_type=jnp.float32)
    return prior_cov - gram
```

```python
import functools

import jax
import jax.numpy as jnp
import numpy as np
from jax import lax
from jax.experimental import pallas as pl
from jax.experimental.pallas import tpu as pltpu
from jax.sharding import PartitionSpec as P


CORES = 2
SLOTS = (
    (
        (((1, 0, 0), 0, 0), ((1, 0, 1), 1, 0), ((1, 0, 2), 2, 0), ((1, 0, 3), 3, 0)),
        (((0, 0, 0), 3, 0), ((0, 0, 1), 0, 0), ((0, 0, 2), 1, 0)),
        (((0, 1, 0), 0, 0), ((0, 1, 1), 1, 0)),
    ),
    (
        (((0, 0, 0), 3, 1), ((0, 0, 2), 0, 1), ((0, 0, 3), 2, 2), ((0, 1, 1), 1, 1)),
        (((0, 1, 0), 0, 1), ((0, 1, 3), 3, 2), ((1, 0, 2), 2, 2)),
    ),
    (
        (((0, 0, 0), 1, 1), ((0, 0, 1), 2, 3), ((0, 0, 2), 3, 5)),
        (((0, 0, 1), 0, 4), ((0, 0, 2), 1, 4), ((0, 0, 3), 2, 4), ((1, 0, 3), 3, 4)),
        (((0, 1, 0), 0, 2), ((0, 1, 2), 2, 5), ((0, 1, 3), 3, 4)),
    ),
    (
        (((0, 0, 0), 1, 5), ((0, 0, 1), 2, 0)),
        (((0, 0, 2), 3, 8), ((0, 0, 3), 2, 8)),
        (((0, 1, 0), 0, 7), ((0, 1, 1), 1, 7), ((0, 1, 2), 2, 4), ((0, 1, 3), 3, 7)),
    ),
)
CHIPS = (2, 2, 4)


def frame(chip, y, x):
    return (chip[0] ^ y, chip[1] ^ x, CHIPS[2] - 1 - chip[2] if y else chip[2])


def index_of(chip, core):
    return ((chip[0] * CHIPS[2] + chip[2]) * CHIPS[1] + chip[1]) * CORES + core


def plan():
    classes = range(CHIPS[2])
    held = [{(0, 0, q): (0, -1)} for q in classes]
    slots, count = [], 0
    for number, slot in enumerate(SLOTS):
        permutes, arrivals = [], []
        for messages in slot:
            count += 1
            pairs, sent = [], {}
            for source, q, array in messages:
                sender = source[2] if source[0] == 0 else CHIPS[2] - 1 - source[2]
                sent[sender] = array
                unit = next(u for u, h in held[sender].items() if h[0] == array)
                arrivals.append((q, frame(unit, source[0], source[1]), count))
                for y in range(CHIPS[0]):
                    for x in range(CHIPS[1]):
                        a, b = frame(source, y, x), frame((0, 0, q), y, x)
                        pairs += [(index_of(a, c), index_of(b, c)) for c in range(CORES)]
            permutes.append((pairs, sent))
        for q, unit, array in arrivals:
            held[q].setdefault(unit, (array, number))
        slots.append(permutes)
    return slots, held


def work():
    slots, held = plan()
    half = CHIPS[2] // CHIPS[0]
    calls = [[[] for _ in range(CHIPS[0] * CHIPS[1] * CHIPS[2] * CORES)] for _ in range(len(slots) + 1)]
    for y in range(CHIPS[0]):
        for x in range(CHIPS[1]):
            for q in range(CHIPS[2]):
                for bx in range(CHIPS[1]):
                    for bz in range(half):
                        (a, s), (b, t) = held[q][0, bx, bz], held[q][1, bx, bz]
                        ready = max(s, t, 0)
                        row = (half - 1 - bz if y else bz) * CHIPS[1] + (bx ^ x)
                        for core in range(CORES):
                            device = index_of(frame((0, 0, q), y, x), core)
                            calls[ready][device].append(((a, 0), (b, 0), row * CORES + core))
                            calls[ready + 1][device].append(((a, 1), (b, 1), row * CORES + 1 - core))
    return [(sorted({k for jobs in call for job in jobs for k in job[:2]}), call) for call in calls]


def split(value):
    high = value.astype(jnp.bfloat16)
    return high, (value - high.astype(jnp.float32)).astype(jnp.bfloat16)


def update(tile, chained, table, own, other, prior, *refs):
    refs = list(refs)
    if chained:
        refs.pop(0)
    *arrays, out, right, high, low, left, before, after, sem = refs
    depth, width = own.shape
    pieces = width // tile
    count = table[0] * pieces

    def place(job):
        j, h = job // pieces, job % pieces
        row = pl.multiple_of(table[3 + 3 * j] * width + h * tile, tile)
        return j, pl.multiple_of(h * tile, tile), row

    def fetch(job, slot):
        j, column, row = place(job)
        for part in range(2):
            chosen = table[1 + 3 * j + part]
            for k, array in enumerate(arrays):
                @pl.when(chosen == k)
                def _(array=array, part=part):
                    pltpu.make_async_copy(
                        array.at[:, pl.ds(column, tile)], left.at[slot, part], sem.at[part, slot]
                    ).start()
        pltpu.make_async_copy(prior.at[pl.ds(row, tile), :], before.at[slot], sem.at[2, slot]).start()

    def store(job, slot):
        row = place(job)[2]
        return pltpu.make_async_copy(after.at[slot], out.at[pl.ds(row, tile), :], sem.at[3, slot])

    def halves(slot):
        return [
            pltpu.make_async_copy(arrays[0].at[:, pl.ds(0, tile)], left.at[slot, part], sem.at[part, slot])
            for part in range(2)
        ] + [pltpu.make_async_copy(prior.at[pl.ds(0, tile), :], before.at[slot], sem.at[2, slot])]

    @pl.when(count > 0)
    def _():
        loads = [
            pltpu.make_async_copy(own, right.at[0], sem.at[4, 0]),
            pltpu.make_async_copy(other, right.at[1], sem.at[4, 1]),
        ]
        for load in loads:
            load.start()
        fetch(0, 0)
        for load in loads:
            load.wait()
        for part in range(2):
            high[pl.ds(part * depth, depth), :], low[pl.ds(part * depth, depth), :] = split(right[part])

    def step(job, carry):
        slot = job & 1

        @pl.when(job + 1 < count)
        def _():
            fetch(job + 1, 1 - slot)

        for load in halves(slot):
            load.wait()

        @pl.when(job >= 2)
        def _():
            store(job - 2, slot).wait()

        dot = functools.partial(
            lax.dot_general,
            dimension_numbers=(((0,), (0,)), ((), ())),
            preferred_element_type=jnp.float32,
        )
        top, rest = split(left[slot].reshape(2 * depth, tile))
        product = dot(top, high[...]) + (dot(top, low[...]) + dot(rest, high[...]))
        after[slot] = before[slot] - product
        store(job, slot).start()
        return carry

    lax.fori_loop(0, count, step, 0)

    @pl.when(count > 1)
    def _():
        store(count - 2, count & 1).wait()

    @pl.when(count > 0)
    def _():
        store(count - 1, (count - 1) & 1).wait()


def call(table, own, other, prior, result, arrays, most):
    depth, width = own.shape
    tile = width // 2
    chained = result is not None
    anywhere = pl.BlockSpec(memory_space=pl.ANY)
    operands = [table, own, other, prior] + ([result] if chained else []) + arrays
    return pl.pallas_call(
        functools.partial(update, tile, chained),
        in_specs=[pl.BlockSpec(memory_space=pltpu.SMEM)] + [anywhere] * (len(operands) - 1),
        out_specs=anywhere,
        out_shape=jax.ShapeDtypeStruct(prior.shape, prior.dtype),
        scratch_shapes=[
            pltpu.VMEM((2, depth, width), jnp.float32),
            pltpu.VMEM((2 * depth, width), jnp.bfloat16),
            pltpu.VMEM((2 * depth, width), jnp.bfloat16),
            pltpu.VMEM((2, 2, depth, tile), jnp.float32),
            pltpu.VMEM((2, tile, width), jnp.float32),
            pltpu.VMEM((2, tile, width), jnp.float32),
            pltpu.SemaphoreType.DMA((5, 2)),
        ],
        input_output_aliases={4: 0} if chained else {},
        compiler_params=pltpu.CompilerParams(vmem_limit_bytes=28 << 20),
        cost_estimate=pl.CostEstimate(
            flops=most * 12 * depth * width * width,
            bytes_accessed=most * 12 * width * width,
            transcendentals=0,
        ),
    )(*operands)


def scheduled(w_slab, prior_cov):
    slots, _ = plan()
    calls = work()
    axes = ("row", "col")
    device = lax.axis_index(axes)
    y, z = lax.axis_index("row"), lax.axis_index("col") // (CHIPS[1] * CORES)
    group = jnp.where(y == 0, z, CHIPS[2] - 1 - z)

    tables, starts = [], []
    for names, jobs in calls:
        most = max(map(len, jobs))
        starts.append(most)
        rows = np.zeros((len(jobs), 1 + 3 * most), np.int32)
        for d, mine in enumerate(jobs):
            rows[d, 0] = len(mine)
            for j, (a, b, row) in enumerate(mine):
                rows[d, 1 + 3 * j : 4 + 3 * j] = names.index(a), names.index(b), row
        tables.append(jnp.asarray(rows)[device])

    partner = [(d, d ^ 1) for d in range(lax.axis_size("row") * lax.axis_size("col"))]
    arrays = [w_slab]
    swapped = {}

    def swap(k):
        if k not in swapped:
            swapped[k] = lax.ppermute(arrays[k], axes, partner)
        return swapped[k]

    result = None
    for number in range(len(slots) + 1):
        brought = []
        if number < len(slots):
            values = []
            for _, sent in slots[number]:
                choice = sorted(set(sent.values()))
                value = arrays[choice[0]]
                for option in choice[1:]:
                    pick = functools.reduce(jnp.logical_or, [group == q for q, a in sent.items() if a == option])
                    value = jnp.where(pick, arrays[option], value)
                values.append(value)
            brought = [lax.ppermute(value, axes, pairs) for value, (pairs, _) in zip(values, slots[number])]
        if number > 0:
            names, _ = calls[number - 1]
            taken = [swap(k) if swapping else arrays[k] for k, swapping in names]
            result = call(tables[number - 1], w_slab, arrays[1], prior_cov, result, taken, starts[number - 1])
            if brought:
                brought, result = lax.optimization_barrier((brought, result))
        elif brought:
            brought = lax.optimization_barrier(brought)
        arrays += brought
    names, _ = calls[-1]
    taken = [swap(k) if swapping else arrays[k] for k, swapping in names]
    return call(tables[-1], w_slab, arrays[1], prior_cov, result, taken, starts[-1])


def from_root(value, axis, source):
    kept = jnp.where(lax.axis_index(axis) == source, value, 0).astype(value.dtype)
    return lax.psum(kept, axis)


def broadcast(w_slab, prior_cov):
    own_block = lax.all_gather(w_slab, "row", axis=0, tiled=True)
    width = own_block.shape[1]
    groups = lax.axis_size("col") // lax.axis_size("row")
    row_index = lax.axis_index("row")
    result = prior_cov
    for step in range(groups):
        slot = jnp.int32(step)
        root = row_index * groups + slot
        received = from_root(own_block, "col", root)
        product = lax.dot_general(
            received,
            own_block,
            (((0,), (0,)), ((), ())),
            precision=lax.Precision.HIGHEST,
            preferred_element_type=jnp.float32,
        )
        start = slot * width
        current = lax.dynamic_slice_in_dim(result, start, width, 0)
        result = lax.dynamic_update_slice_in_dim(result, current - product, start, 0)
    return result


def solution(mesh):
    sizes = (mesh.shape["row"], mesh.shape["col"])
    fits = sizes == (CHIPS[0], CHIPS[1] * CHIPS[2] * CORES)
    return jax.shard_map(
        scheduled if fits else broadcast,
        mesh=mesh,
        in_specs=(P("row", "col"), P("row", "col")),
        out_specs=P("row", "col"),
        check_vma=False,
    )
```

```python
import functools

import jax
import jax.numpy as jnp
import numpy as np
from jax import lax
from jax.experimental import pallas as pl
from jax.experimental.pallas import tpu as pltpu
from jax.sharding import PartitionSpec as P


CORES = 2
SLOTS = (
    (
        (((1, 0, 0), 0, 0), ((1, 0, 1), 1, 0), ((1, 0, 2), 2, 0), ((1, 0, 3), 3, 0)),
        (((0, 0, 0), 3, 0), ((0, 0, 1), 0, 0), ((0, 0, 3), 1, 0), ((0, 0, 2), 2, None)),
        (((0, 1, 0), 0, 0), ((0, 1, 1), 1, 0), ((0, 1, 2), 2, 0), ((0, 1, 3), 3, None)),
    ),
    (
        (((0, 0, 0), 3, 1), ((0, 0, 1), 0, 1), ((0, 0, 2), 1, 0), ((0, 0, 3), 2, 2)),
        (((0, 1, 0), 0, 1), ((0, 1, 3), 3, 2), ((1, 0, 1), 1, 3), ((1, 0, 2), 2, 2)),
    ),
    (
        (((0, 0, 0), 1, 3), ((0, 0, 1), 3, 0), ((0, 0, 2), 0, 3), ((0, 0, 3), 2, 5)),
        (((1, 0, 0), 0, None), ((1, 0, 1), 1, None), ((1, 0, 2), 2, 4), ((1, 0, 3), 3, None)),
        (((0, 1, 0), 0, 4), ((0, 1, 1), 1, None), ((0, 1, 2), 2, 5), ((0, 1, 3), 3, 4)),
    ),
    (
        (((0, 0, 1), 0, None), ((0, 0, 2), 1, 5), ((0, 0, 3), 2, 6), ((1, 0, 3), 3, 6)),
        (((0, 0, 0), 1, 5), ((0, 0, 1), 2, 3), ((0, 0, 2), 3, 7), ((1, 0, 0), 0, None)),
        (((0, 1, 0), 0, 2), ((0, 1, 1), 1, 6), ((0, 1, 2), 2, 7), ((0, 1, 3), 3, 6)),
    ),
)
CHIPS = (2, 2, 4)


def frame(chip, y, x):
    return (chip[0] ^ y, chip[1] ^ x, CHIPS[2] - 1 - chip[2] if y else chip[2])


def index_of(chip, core):
    return ((chip[0] * CHIPS[2] + chip[2]) * CHIPS[1] + chip[1]) * CORES + core


def plan():
    classes = range(CHIPS[2])
    held = [{(0, 0, q): (0, -1)} for q in classes]
    slots, count = [], 0
    for number, slot in enumerate(SLOTS):
        permutes, arrivals = [], []
        for messages in slot:
            count += 1
            pairs, sent = [], {}
            for source, q, array in messages:
                if array is not None:
                    sender = source[2] if source[0] == 0 else CHIPS[2] - 1 - source[2]
                    sent[sender] = array
                    unit = next(u for u, h in held[sender].items() if h[0] == array)
                    arrivals.append((q, frame(unit, source[0], source[1]), count))
                for y in range(CHIPS[0]):
                    for x in range(CHIPS[1]):
                        a, b = frame(source, y, x), frame((0, 0, q), y, x)
                        pairs += [(index_of(a, c), index_of(b, c ^ (a == b))) for c in range(CORES)]
            permutes.append((pairs, sent))
        for q, unit, array in arrivals:
            held[q].setdefault(unit, (array, number))
        slots.append(permutes)
    return slots, held


CALLS = ((1, (0,), ()), (2, (1,), (0,)), (3, (2,), (1,)), (3, (), (2,)), (4, (3,), ()), (4, (), (3,)))


def work():
    _, held = plan()
    half = CHIPS[2] // CHIPS[0]
    calls = [[[] for _ in range(CHIPS[0] * CHIPS[1] * CHIPS[2] * CORES)] for _ in CALLS]
    for y in range(CHIPS[0]):
        for x in range(CHIPS[1]):
            for q in range(CHIPS[2]):
                for bx in range(CHIPS[1]):
                    for bz in range(half):
                        (a, s), (b, t) = held[q][0, bx, bz], held[q][1, bx, bz]
                        ready = max(s, t, 0)
                        row = (half - 1 - bz if y else bz) * CHIPS[1] + (bx ^ x)
                        for core in range(CORES):
                            device = index_of(frame((0, 0, q), y, x), core)
                            for swapped in range(CORES):
                                n = next(n for n, call in enumerate(CALLS) if ready in call[1 + swapped])
                                calls[n][device].append(((a, swapped), (b, swapped), row * CORES + (core ^ swapped)))
    return [(sorted({k for jobs in call for job in jobs for k in job[:2]}), call) for call in calls]


def split(value):
    high = value.astype(jnp.bfloat16)
    return high, (value - high.astype(jnp.float32)).astype(jnp.bfloat16)


def update(tile, chained, table, own, other, prior, *refs):
    refs = list(refs)
    if chained:
        refs.pop(0)
    *arrays, out, right, high, low, left, before, after, sem = refs
    depth, width = own.shape
    pieces = width // tile
    count = table[0] * pieces

    def place(job):
        j, h = job // pieces, job % pieces
        row = pl.multiple_of(table[3 + 3 * j] * width + h * tile, tile)
        return j, pl.multiple_of(h * tile, tile), row

    def fetch(job, slot):
        j, column, row = place(job)
        for part in range(2):
            chosen = table[1 + 3 * j + part]
            for k, array in enumerate(arrays):
                @pl.when(chosen == k)
                def _(array=array, part=part):
                    pltpu.make_async_copy(
                        array.at[:, pl.ds(column, tile)], left.at[slot, part], sem.at[part, slot]
                    ).start()
        pltpu.make_async_copy(prior.at[pl.ds(row, tile), :], before.at[slot], sem.at[2, slot]).start()

    def store(job, slot):
        row = place(job)[2]
        return pltpu.make_async_copy(after.at[slot], out.at[pl.ds(row, tile), :], sem.at[3, slot])

    def halves(slot):
        return [
            pltpu.make_async_copy(arrays[0].at[:, pl.ds(0, tile)], left.at[slot, part], sem.at[part, slot])
            for part in range(2)
        ] + [pltpu.make_async_copy(prior.at[pl.ds(0, tile), :], before.at[slot], sem.at[2, slot])]

    @pl.when(count > 0)
    def _():
        loads = [
            pltpu.make_async_copy(own, right.at[0], sem.at[4, 0]),
            pltpu.make_async_copy(other, right.at[1], sem.at[4, 1]),
        ]
        for load in loads:
            load.start()
        fetch(0, 0)
        for load in loads:
            load.wait()
        for part in range(2):
            high[pl.ds(part * depth, depth), :], low[pl.ds(part * depth, depth), :] = split(right[part])

    def step(job, carry):
        slot = job & 1

        @pl.when(job + 1 < count)
        def _():
            fetch(job + 1, 1 - slot)

        for load in halves(slot):
            load.wait()

        @pl.when(job >= 2)
        def _():
            store(job - 2, slot).wait()

        dot = functools.partial(
            lax.dot_general,
            dimension_numbers=(((0,), (0,)), ((), ())),
            preferred_element_type=jnp.float32,
        )
        top, rest = split(left[slot].reshape(2 * depth, tile))
        product = dot(top, high[...]) + (dot(top, low[...]) + dot(rest, high[...]))
        after[slot] = before[slot] - product
        store(job, slot).start()
        return carry

    lax.fori_loop(0, count, step, 0)

    @pl.when(count > 1)
    def _():
        store(count - 2, count & 1).wait()

    @pl.when(count > 0)
    def _():
        store(count - 1, (count - 1) & 1).wait()


def call(table, own, other, prior, result, arrays, most):
    depth, width = own.shape
    tile = width // 2
    chained = result is not None
    anywhere = pl.BlockSpec(memory_space=pl.ANY)
    operands = [table, own, other, prior] + ([result] if chained else []) + arrays
    return pl.pallas_call(
        functools.partial(update, tile, chained),
        in_specs=[pl.BlockSpec(memory_space=pltpu.SMEM)] + [anywhere] * (len(operands) - 1),
        out_specs=anywhere,
        out_shape=jax.ShapeDtypeStruct(prior.shape, prior.dtype),
        scratch_shapes=[
            pltpu.VMEM((2, depth, width), jnp.float32),
            pltpu.VMEM((2 * depth, width), jnp.bfloat16),
            pltpu.VMEM((2 * depth, width), jnp.bfloat16),
            pltpu.VMEM((2, 2, depth, tile), jnp.float32),
            pltpu.VMEM((2, tile, width), jnp.float32),
            pltpu.VMEM((2, tile, width), jnp.float32),
            pltpu.SemaphoreType.DMA((5, 2)),
        ],
        input_output_aliases={4: 0} if chained else {},
        compiler_params=pltpu.CompilerParams(vmem_limit_bytes=19 << 20),
        cost_estimate=pl.CostEstimate(
            flops=most * 12 * depth * width * width,
            bytes_accessed=most * 12 * width * width,
            transcendentals=0,
        ),
    )(*operands)


def scheduled(w_slab, prior_cov):
    slots, _ = plan()
    calls = work()
    axes = ("row", "col")
    device = lax.axis_index(axes)
    y, z = lax.axis_index("row"), lax.axis_index("col") // (CHIPS[1] * CORES)
    group = jnp.where(y == 0, z, CHIPS[2] - 1 - z)

    most = [max(map(len, jobs)) for _, jobs in calls]
    rows = np.zeros((len(calls[0][1]), len(calls), 1 + 3 * max(most)), np.int32)
    for n, (names, jobs) in enumerate(calls):
        for d, mine in enumerate(jobs):
            rows[d, n, 0] = len(mine)
            for j, (a, b, row) in enumerate(mine):
                rows[d, n, 1 + 3 * j : 4 + 3 * j] = names.index(a), names.index(b), row
    tables = jnp.asarray(rows)[device]

    partner = [(d, d ^ 1) for d in range(lax.axis_size("row") * lax.axis_size("col"))]
    arrays = [w_slab]
    for slot in slots:
        pieces, own_group = lax.optimization_barrier((list(arrays), group))
        brought = []
        for pairs, sent in slot:
            choice = sorted(set(sent.values()))
            value = pieces[choice[0]]
            for option in choice[1:]:
                pick = functools.reduce(jnp.logical_or, [own_group == q for q, a in sent.items() if a == option])
                value = jnp.where(pick, pieces[option], value)
            brought.append(lax.ppermute(value, axes, pairs))
        arrays = arrays + brought

    swapped = {}

    def swap(k):
        if k not in swapped:
            swapped[k] = lax.ppermute(arrays[k], axes, partner)
        return swapped[k]

    result = None
    for n, (names, _) in enumerate(calls):
        taken = [swap(k) if swapping else arrays[k] for k, swapping in names]
        result = call(tables[n], w_slab, arrays[1], prior_cov, result, taken, most[n])
    return result


def from_root(value, axis, source):
    kept = jnp.where(lax.axis_index(axis) == source, value, 0).astype(value.dtype)
    return lax.psum(kept, axis)


def broadcast(w_slab, prior_cov):
    own_block = lax.all_gather(w_slab, "row", axis=0, tiled=True)
    width = own_block.shape[1]
    groups = lax.axis_size("col") // lax.axis_size("row")
    row_index = lax.axis_index("row")
    result = prior_cov
    for step in range(groups):
        slot = jnp.int32(step)
        root = row_index * groups + slot
        received = from_root(own_block, "col", root)
        product = lax.dot_general(
            received,
            own_block,
            (((0,), (0,)), ((), ())),
            precision=lax.Precision.HIGHEST,
            preferred_element_type=jnp.float32,
        )
        start = slot * width
        current = lax.dynamic_slice_in_dim(result, start, width, 0)
        result = lax.dynamic_update_slice_in_dim(result, current - product, start, 0)
    return result


def solution(mesh):
    sizes = (mesh.shape["row"], mesh.shape["col"])
    fits = sizes == (CHIPS[0], CHIPS[1] * CHIPS[2] * CORES)

    def body(w_slab, prior_cov):
        return (scheduled if fits else broadcast)(w_slab, prior_cov)

    return jax.shard_map(
        body,
        mesh=mesh,
        in_specs=(P("row", "col"), P("row", "col")),
        out_specs=P("row", "col"),
        check_vma=False,
    )
```
